32 devices in a mesh: req: 16 (over z, y, x), tp: 2 (over core).
Axes of the slice: x: 2, y: 2, z: 4, core: 2. Of those that a mesh axis runs over, the one named last changes fastest.
Arguments:
- hidden: bfloat16 [16, 32, 2048], P('req', 'tp'), may hold values from -4.5 to 4.5
- norm_gain: float32 [2048], replicated, may hold values from 0.1 to 1.9
- embedding: bfloat16 [16384, 2048], P(('req', 'tp')), may hold values from -0.79549513 to 0.79549513
- target_ids: int32 [16, 32], P('req', 'tp'), may hold values from 0 to 16383
- lengths: int32 [16], P('req'), may hold values from 1 to 32, 320 in all
- response_mask: int32 [16, 32], P('req', 'tp'), may hold values 0 or 1
Outputs:
- logprob: float32 [16, 32], P('req', 'tp')
- entropy: float32 [16, 32], P('req', 'tp')
The draws below stay inside these ranges and needn't reach their ends.
All inputs are finite; a program needn't handle non-finite values. No bound on the sum of `lengths` or of `response_mask` on one device may be relied on, other than what follows from the above.
Results may differ from the reference program's by a relative error of at most 0.0027.
Values may be sent and summed in bfloat16 or wider, within the bound.
A program may use at most 64 MiB of HBM per device.

```python
import math
import jax
import jax.numpy as jnp
import numpy as np
from jax import lax

D = 2048
VOC_DEV = 512
CAP = 32
SEQS = 16
TOKENS = 512
VOCAB = 16384
N_REQ = 16
N_TP = 2


def unit_row(key, vocab_id):
    inner = jax.random.fold_in(jax.random.fold_in(key, 71), vocab_id)
    return jax.random.truncated_normal(inner, -4.0, 4.0, (D,), jnp.float32)


def draw_target_ids(key, part):
    return jax.random.randint(jax.random.fold_in(key, 29), (SEQS, CAP), 0, VOCAB, dtype=jnp.int32)


def draw_embedding(key, part):
    units = jax.vmap(lambda v: unit_row(key, v))(jnp.arange(VOCAB, dtype=jnp.int32))
    spread = 0.8
    logs = jax.random.uniform(jax.random.fold_in(key, 73), (VOCAB, 1), jnp.float32, -spread, spread)
    return (units * jnp.exp(logs) * (3.0 / math.sqrt(D))).astype(jnp.bfloat16)


def draw_hidden(key, part):
    targets = draw_target_ids(key, part).reshape(-1)
    units = jax.vmap(lambda v: unit_row(key, v))(targets).reshape(SEQS, CAP, D)
    weight = 4.0 / math.sqrt(D)
    noise = jax.random.truncated_normal(jax.random.fold_in(key, 83), -4.0, 4.0, (SEQS, CAP, D), jnp.float32)
    return (weight * units + noise).astype(jnp.bfloat16)


def plant(drawn, key, smallest, top_value):
    shape = drawn.shape
    spot = [jax.random.randint(jax.random.fold_in(key, axis), (), 0, shape[axis]) for axis in range(len(shape))]
    drawn = drawn.at[tuple(spot)].set(smallest)
    longest = shape.index(max(shape))
    spot[longest] = (spot[longest] + 1) % shape[longest]
    return drawn.at[tuple(spot)].set(top_value)


def length_profile(amount, total, bound, lean):
    loads = [(1 << 20) // math.isqrt(standing ** lean) + 1 for standing in range(2, amount + 1)]
    surplus, given = total - bound - (amount - 1), [1] * (amount - 1)
    while surplus > 0:
        candidates = [i for i in range(amount - 1) if given[i] < bound]
        whole, budget = sum([loads[i] for i in candidates]), surplus
        for i in candidates:
            extra = min(bound - given[i], max(1, budget * loads[i] // whole), surplus)
            given[i] = given[i] + extra
            surplus = surplus - extra
    return np.array([bound] + given)


def ragged(key, amount, total, limit, lean):
    if amount == 2:
        one = jax.random.randint(key, (), max(1, total - limit), min(limit, total - 1) + 1)
        return jnp.stack([one, total - one])
    sizes = jnp.asarray(length_profile(amount, total, limit, lean), jnp.int32)
    pairs = (amount - 1) // 2
    giver, receiver = sizes[1:1 + 2 * pairs:2], sizes[2:2 + 2 * pairs:2]
    slack = jnp.minimum(giver - 1, limit - receiver)
    moved = jax.random.randint(jax.random.fold_in(key, 1), (pairs,), 0, 1 << 20) % (slack + 1)
    sizes = sizes.at[1:1 + 2 * pairs:2].set(giver - moved).at[2:2 + 2 * pairs:2].set(receiver + moved)
    return sizes[jax.random.permutation(jax.random.fold_in(key, 2), amount)]


def setup_inputs(seed: int = 0) -> dict:
    key_list = jax.random.split(jax.random.key(seed), 7)
    hidden = draw_hidden(jax.random.fold_in(key_list[6], 71), 0)
    norm_gain = jnp.clip(1.0 + 0.18 * jax.random.normal(key_list[1], (D,), jnp.float32), 0.1, 1.9)
    embedding = draw_embedding(jax.random.fold_in(key_list[6], 71), 0)
    target_ids = draw_target_ids(jax.random.fold_in(key_list[6], 71), 0)
    lengths = ragged(key_list[4], SEQS, N_REQ * CAP * 5 // 8, CAP, 1).astype(jnp.int32)
    response_mask = plant((jax.random.randint(key_list[5], (SEQS, CAP), 0, 4) < 3).astype(jnp.int32), jax.random.fold_in(key_list[5], 1), 0, 1)
    return {"hidden": hidden, "norm_gain": norm_gain, "embedding": embedding, "target_ids": target_ids, "lengths": lengths, "response_mask": response_mask}


def reference(hidden, norm_gain, embedding, target_ids, lengths, response_mask):
    rows = hidden.astype(jnp.float32).reshape(TOKENS, D)
    scale = lax.rsqrt(lax.optimization_barrier(jnp.mean(rows * rows, axis=1, keepdims=True)) + 1e-06)
    normed = (rows * scale * norm_gain[None, :]).astype(jnp.bfloat16)
    targets = target_ids.reshape(TOKENS)
    block_rows = VOC_DEV * N_TP
    blocks = embedding.reshape(VOCAB // block_rows, block_rows, D)
    starts = (jnp.arange(VOCAB // block_rows) * block_rows).astype(jnp.int32)

    def visit(carry, inputs):
        table, start = inputs
        raw = lax.dot_general(normed, table, (((1,), (1,)), ((), ())), preferred_element_type=jnp.float32)
        logits = 30.0 * jnp.tanh(raw / 30.0)
        expo = jnp.exp(logits)
        ident = start + lax.broadcasted_iota(jnp.int32, (1, block_rows), 1)
        hit = jnp.where(ident == targets[:, None], logits, jnp.float32(0.0))
        return ((carry[0] + lax.optimization_barrier(jnp.sum(expo, axis=1)), carry[1] + lax.optimization_barrier(jnp.sum(expo * logits, axis=1)), carry[2] + lax.optimization_barrier(jnp.sum(hit, axis=1))), None)
    zeros = jnp.zeros((TOKENS,), jnp.float32)
    (total, moment, picked), unused = lax.scan(visit, (zeros, zeros, zeros), (blocks, starts))
    lse = jnp.log(total)
    position = lax.broadcasted_iota(jnp.int32, (SEQS, CAP), 1)
    scored = (response_mask == 1) & (position < lengths[:, None])
    logprob = jnp.where(scored, (picked - lse).reshape(SEQS, CAP), jnp.float32(0.0))
    entropy = jnp.where(scored, (lse - moment / total).reshape(SEQS, CAP), jnp.float32(0.0))
    return (logprob, entropy)
```

```python
import functools

import jax
import jax.numpy as jnp
from jax import lax
from jax.experimental import pallas as pl
from jax.experimental.pallas import tpu as pltpu
from jax.sharding import PartitionSpec as P

MESH = pl.DeviceIdType.MESH
SPECS = dict(
    in_specs=(
        P("req", "tp", None),
        P(),
        P(("req", "tp"), None),
        P("req", "tp"),
        P("req"),
        P("req", "tp"),
    ),
    out_specs=(P("req", "tp"), P("req", "tp")),
    check_vma=False,
)


def vocab_sums(states, targets, table, vocab_start):
    raw = lax.dot_general(
        states, table, (((1,), (1,)), ((), ())), preferred_element_type=jnp.float32
    )
    logits = 30.0 * jnp.tanh(raw / 30.0)
    expo = jnp.exp(logits)
    ident = vocab_start + lax.broadcasted_iota(jnp.int32, (1, table.shape[0]), 1)
    hit = jnp.where(ident == targets[:, None], logits, jnp.float32(0.0))
    return (jnp.sum(expo, axis=1), jnp.sum(expo * logits, axis=1), jnp.sum(hit, axis=1))


def on_device(hidden, norm_gain, embedding, target_ids, lengths, response_mask):
    seq_here, slots, width = hidden.shape
    rows = hidden.reshape(seq_here * slots, width).astype(jnp.float32)
    scale = lax.rsqrt(jnp.mean(rows * rows, axis=1, keepdims=True) + 1e-06)
    normed = (rows * scale * norm_gain[None, :]).astype(jnp.bfloat16)
    targets = target_ids.reshape(seq_here * slots)
    vocab_start = lax.axis_index(("req", "tp")) * embedding.shape[0]
    sums = vocab_sums(
        lax.all_gather(normed, ("req", "tp"), axis=0, tiled=True),
        lax.all_gather(targets, ("req", "tp"), axis=0, tiled=True),
        embedding,
        vocab_start,
    )
    total, moment, picked = (
        lax.psum_scatter(s, ("req", "tp"), scatter_dimension=0, tiled=True) for s in sums
    )
    lse = jnp.log(total)
    position = lax.axis_index("tp") * slots + lax.broadcasted_iota(jnp.int32, (seq_here, slots), 1)
    scored = (response_mask == 1) & (position < lengths[:, None])
    logprob = jnp.where(scored, (picked - lse).reshape(seq_here, slots), jnp.float32(0.0))
    entropy = jnp.where(scored, (lse - moment / total).reshape(seq_here, slots), jnp.float32(0.0))
    return (logprob, entropy)


PARTS = 1
RELAYED = ()


def J(b, a, area, s):
    return s * 8 + b * 4 + a * 2 + area


def kernel(slots, hidden_hbm, gain_hbm, target_hbm, mask_hbm, length_hbm, emb_hbm, out_ref,
           hidden, gain, target_row, mask, length, emb, X, part, R,
           load_sem, z_sem, a_sem, b_sem, c_sem, p_sem, xr, rs, rr):
    width = hidden.shape[1]
    voc = emb.shape[0]
    q, c = lax.axis_index("req"), lax.axis_index("tp")
    x, y, z = q % 2, (q // 2) % 2, q // 4
    order = (z, 1 + z % 2, 2 - 2 * (z % 2) + z // 2, 3 - 3 * (z // 2))

    def device(nz, fa, fb, core):
        fx, fy = fa * (1 - c) + fb * c, fb * (1 - c) + fa * c
        nx, ny = x + fx * (1 - 2 * x), y + fy * (1 - 2 * y)
        return (nz * 4 + ny * 2 + nx, core)

    column = [device(order[i], 0, 0, c) for i in range(1, 4)]
    a_side, b_side, partner = device(z, 1, 0, c), device(z, 0, 1, c), device(z, 0, 0, 1 - c)
    diagonal = device(z, 1, 1, c)
    near = column + [a_side, b_side, diagonal, partner]

    barrier = pltpu.get_barrier_semaphore()

    for d in near:
        pl.semaphore_signal(barrier, inc=1, device_id=d, device_id_type=MESH)

    loads = [pltpu.make_async_copy(src, dst, load_sem.at[i]) for i, (src, dst) in enumerate(
        ((hidden_hbm, hidden), (gain_hbm, gain), (target_hbm, target_row), (mask_hbm, mask),
         (length_hbm, length), (emb_hbm, emb)))]
    for copy in loads:
        copy.start()
    for copy in loads[:3]:
        copy.wait()
    rows = hidden[...].astype(jnp.float32)
    scale = lax.rsqrt(jnp.mean(rows * rows, axis=1, keepdims=True) + 1e-06)
    own = pl.ds(pl.multiple_of(z * 8 * slots, slots), slots)
    X[own, 0:width] = (rows * scale * gain[...]).astype(jnp.bfloat16)
    tgt = jnp.broadcast_to(target_row[...], (slots, slots))
    eye = lax.broadcasted_iota(jnp.int32, (slots, slots), 0) == lax.broadcasted_iota(
        jnp.int32, (slots, slots), 1)
    tcol = jnp.sum(jnp.where(eye, tgt, 0).astype(jnp.float32), axis=1, keepdims=True)
    high = jnp.floor(tcol * (1.0 / 256.0))
    low = tcol - high * 256.0
    lane = lax.broadcasted_iota(jnp.int32, (slots, 128), 1)
    X[own, width:width + 128] = jnp.where(
        lane == 0, high, jnp.where(lane == 1, low, 0.0)).astype(jnp.bfloat16)
    pl.semaphore_wait(barrier, len(near))

    piece = slots // PARTS

    def block(slot, h):
        return X.at[pl.ds(pl.multiple_of(slot * slots + h * piece, piece), piece), :]

    def copy_of(src, dst, h, send_sem, dev):
        return pltpu.make_async_remote_copy(
            src_ref=block(src, h), dst_ref=block(dst, h), send_sem=send_sem,
            recv_sem=xr.at[dst, h], device_id=dev, device_id_type=MESH)

    def copies(b, a, i, h):
        s, here, out = order[i], J(b, a, 0, order[i]), []
        if b + a + i == 0:
            for n in (0, 1, 2):
                out.append(copy_of(here, here, h, z_sem.at[n, h], column[n]))
        if b + a == 0:
            if i not in RELAYED:
                out.append(copy_of(here, J(1, 1, 0, s), h, c_sem.at[i, h], diagonal))
            out.append(copy_of(here, J(0, 1, 0, s), h, a_sem.at[i, h], a_side))
            out.append(copy_of(here, J(1, 0, 0, s), h, b_sem.at[i, h], b_side))
        if b == 0 and a == 1 and i in RELAYED:
            out.append(copy_of(here, J(1, 1, 0, s), h, c_sem.at[i, h], b_side))
        out.append(copy_of(here, J(b, a, 1, s), h, p_sem.at[i * 4 + b * 2 + a, h], partner))
        return out

    sends = []

    def forward(b, a, i, h):
        for copy in copies(b, a, i, h):
            copy.start()
            sends.append(copy)

    def arrived(slot, h):
        copy_of(slot, slot, h, p_sem.at[0, h], partner).wait_recv()

    def relay(b, a, i):
        for h in range(PARTS):
            arrived(J(b, a, 0, order[i]), h)
            forward(b, a, i, h)

    start = ((q * 2 + c) * voc).astype(jnp.float32)
    outs = []

    def group(i):
        for b in range(2):
            for a in range(2):
                for h in range(PARTS):
                    arrived(J(b, a, 1, order[i]), h)
        toks = 8 * slots
        base = pl.multiple_of(order[i] * toks, toks)
        pick = lax.broadcasted_iota(jnp.int32, (8, 128), 1)
        pick = jnp.where(pick == 0, 256.0, jnp.where(pick == 1, 1.0, 0.0)).astype(jnp.bfloat16)
        target = lax.dot_general(
            pick, X[pl.ds(base, toks), width:width + 128], (((1,), (1,)), ((), ())),
            preferred_element_type=jnp.float32)[0:1, :] - start
        raw = lax.dot_general(
            emb[...], X[pl.ds(base, toks), 0:width], (((1,), (1,)), ((), ())),
            preferred_element_type=jnp.float32)
        logits = 30.0 * jnp.tanh(raw / 30.0)
        expo = jnp.exp(logits)
        ident = lax.broadcasted_iota(jnp.int32, (voc, toks), 0).astype(jnp.float32)
        part[i, 0:1, :] = jnp.sum(expo, axis=0, keepdims=True)
        part[i, 1:2, :] = jnp.sum(expo * logits, axis=0, keepdims=True)
        part[i, 2:3, :] = jnp.sum(jnp.where(ident == target, logits, 0.0), axis=0, keepdims=True)
        part[i, 3:4, :] = jnp.zeros((1, toks), jnp.float32)
        for k in range(7, -1, -1):
            if i + k == 0:
                continue
            b, a, area = k // 4, k // 2 % 2, k % 2
            fa, fb = (a, b) if area == 0 else (b, a)
            copy = pltpu.make_async_remote_copy(
                src_ref=part.at[i], dst_ref=R.at[z * 8 + k], send_sem=rs.at[i * 8 + k],
                recv_sem=rr.at[z * 8 + k],
                device_id=device(order[i], fa, fb, c if area == 0 else 1 - c),
                device_id_type=MESH)
            copy.start()
            outs.append((copy, order[i] * 8 + k))

    for h in range(PARTS):
        forward(0, 0, 0, h)
    relay(0, 0, 1)
    relay(0, 1, 0)
    relay(1, 0, 0)
    relay(0, 0, 2)
    relay(1, 1, 0)
    relay(0, 0, 3)
    for copy in loads[3:]:
        copy.wait()
    group(0)
    relay(0, 1, 1)
    relay(1, 0, 1)
    relay(1, 1, 1)
    relay(0, 1, 2)
    relay(1, 0, 2)
    relay(1, 1, 2)
    group(1)
    relay(0, 1, 3)
    relay(1, 0, 3)
    relay(1, 1, 3)
    group(2)
    group(3)
    for _, slot in outs:
        pltpu.make_async_remote_copy(
            src_ref=part.at[0], dst_ref=R.at[slot], send_sem=rs.at[0], recv_sem=rr.at[slot],
            device_id=partner, device_id_type=MESH).wait_recv()
    R[z * 8] = part[0]
    home = lax.broadcasted_iota(jnp.int32, (4, 8 * slots), 1) // slots
    acc = jnp.zeros((4, 8 * slots), jnp.float32)
    for k in range(8):
        acc = acc + jnp.where(home == k, (R[k] + R[8 + k]) + (R[16 + k] + R[24 + k]), 0.0)
    for shift in (64, 32, 16):
        acc = acc + pltpu.roll(acc, shift, 1)
    total, moment, picked = (acc[i:i + 1, 0:slots] for i in range(3))
    lse = jnp.log(total)
    position = c * slots + lax.broadcasted_iota(jnp.int32, (1, slots), 1)
    scored = (mask[...] == 1) & (position < length[...])
    out_ref[0:1, :] = jnp.where(scored, picked - lse, 0.0)
    out_ref[1:2, :] = jnp.where(scored, lse - moment / total, 0.0)

    for copy in sends:
        copy.wait_send()
    for copy, _ in outs:
        copy.wait_send()


def fused(hidden, norm_gain, embedding, target_ids, lengths, response_mask):
    _, slots, width = hidden.shape
    voc = embedding.shape[0]
    anywhere = pl.BlockSpec(memory_space=pl.ANY)
    dma = pltpu.SemaphoreType.DMA
    out = pl.pallas_call(
        functools.partial(kernel, slots),
        out_shape=pltpu.VMEM((2, slots), jnp.float32),
        in_specs=[anywhere] * 6,
        out_specs=pl.BlockSpec(memory_space=pltpu.VMEM),
        scratch_shapes=[
            pltpu.VMEM((slots, width), jnp.bfloat16),
            pltpu.VMEM((1, width), jnp.float32),
            pltpu.VMEM((1, slots), jnp.int32),
            pltpu.VMEM((1, slots), jnp.int32),
            pltpu.VMEM((1, 1), jnp.int32),
            pltpu.VMEM((voc, width), jnp.bfloat16),
            pltpu.VMEM((32 * slots, width + 128), jnp.bfloat16),
            pltpu.VMEM((4, 4, 8 * slots), jnp.float32),
            pltpu.VMEM((32, 4, 8 * slots), jnp.float32),
            dma((6,)), dma((3, PARTS)), dma((4, PARTS)), dma((4, PARTS)), dma((4, PARTS)),
            dma((16, PARTS)), dma((32, PARTS)), dma((32,)), dma((32,)),
        ],
        compiler_params=pltpu.CompilerParams(collective_id=0, has_side_effects=True),
    )(hidden.reshape(slots, width), norm_gain.reshape(1, width), target_ids, response_mask,
      lengths.reshape(1, 1), embedding)
    return (out[0:1], out[1:2])


def solution(mesh):
    body = fused if dict(mesh.shape) == {"req": 16, "tp": 2} else on_device
    return jax.shard_map(body, mesh=mesh, **SPECS)
```

```python
import functools
import math

import jax
import jax.numpy as jnp
from jax import lax
from jax.experimental import pallas as pl
from jax.experimental.pallas import tpu as pltpu
from jax.sharding import PartitionSpec as P

MESH = pl.DeviceIdType.MESH
SPECS = dict(
    in_specs=(
        P("req", "tp", None),
        P(),
        P(("req", "tp"), None),
        P("req", "tp"),
        P("req"),
        P("req", "tp"),
    ),
    out_specs=(P("req", "tp"), P("req", "tp")),
    check_vma=False,
)


def vocab_sums(states, targets, table, vocab_start):
    raw = lax.dot_general(
        states, table, (((1,), (1,)), ((), ())), preferred_element_type=jnp.float32
    )
    logits = 30.0 * jnp.tanh(raw / 30.0)
    expo = jnp.exp(logits)
    ident = vocab_start + lax.broadcasted_iota(jnp.int32, (1, table.shape[0]), 1)
    hit = jnp.where(ident == targets[:, None], logits, jnp.float32(0.0))
    return (jnp.sum(expo, axis=1), jnp.sum(expo * logits, axis=1), jnp.sum(hit, axis=1))


def on_device(hidden, norm_gain, embedding, target_ids, lengths, response_mask):
    seq_here, slots, width = hidden.shape
    rows = hidden.reshape(seq_here * slots, width).astype(jnp.float32)
    scale = lax.rsqrt(jnp.mean(rows * rows, axis=1, keepdims=True) + 1e-06)
    normed = (rows * scale * norm_gain[None, :]).astype(jnp.bfloat16)
    targets = target_ids.reshape(seq_here * slots)
    vocab_start = lax.axis_index(("req", "tp")) * embedding.shape[0]
    sums = vocab_sums(
        lax.all_gather(normed, ("req", "tp"), axis=0, tiled=True),
        lax.all_gather(targets, ("req", "tp"), axis=0, tiled=True),
        embedding,
        vocab_start,
    )
    total, moment, picked = (
        lax.psum_scatter(s, ("req", "tp"), scatter_dimension=0, tiled=True) for s in sums
    )
    lse = jnp.log(total)
    position = lax.axis_index("tp") * slots + lax.broadcasted_iota(jnp.int32, (seq_here, slots), 1)
    scored = (response_mask == 1) & (position < lengths[:, None])
    logprob = jnp.where(scored, (picked - lse).reshape(seq_here, slots), jnp.float32(0.0))
    entropy = jnp.where(scored, (lse - moment / total).reshape(seq_here, slots), jnp.float32(0.0))
    return (logprob, entropy)


EXP2 = 30.0 / math.log(2.0)

END = (
    (0, 0, 0, "a"), (0, 0, 0, 2), (0, 0, 0, "b"), (0, 0, 0, "d"), (0, 0, 0, 1), (0, 1, 0),
    (0, 0, 1), (0, 0, 1, "d"), (1, 0, 0), (1, 0, 0, 1), (0, 0, 1, "b"), (0, 0, 2),
    (0, 0, 2, "a"), (0, 0, 2, "b"), (0, 0, 2, 1), (1, 1, 0), (1, 1, 1), (1, 1, 1, 2), (0, 0, 3),
    (0, 0, 3, "d"), (1, 0, 1), (0, 1, 2), (0, 1, 2, "b"), (1, 0, 2), (0, 1, 1), (1, 0, 3),
    (1, 1, 3), (1, 1, 2), (0, 1, 3),
)
MID = (
    (0, 0, 0, 1), (0, 0, 0, "b"), (0, 0, 0, "a"), (0, 0, 0, 3), (1, 0, 0), (1, 0, 0, "a"),
    (0, 1, 0), (0, 1, 0, 2), (0, 0, 3), (0, 0, 3, 1), (0, 0, 3, "b"), (0, 0, 1), (0, 0, 1, "a"),
    (0, 1, 0, 1), (1, 0, 0, 2), (1, 1, 0), (0, 0, 3, "a"), (1, 0, 3), (1, 0, 3, 1), (0, 1, 2),
    (1, 0, 1), (1, 0, 1, "a"), (1, 0, 3, "a"), (0, 1, 1), (0, 1, 3), (0, 1, 3, 1), (1, 0, 2),
    (0, 0, 2), (1, 1, 1), (1, 1, 3), (1, 1, 2),
)
SPLIT = (25, 29)
SENDS = (30, 32)


def J(b, a, area, s):
    return s * 8 + b * 4 + a * 2 + area


def kernel(slots, hidden_hbm, gain_hbm, target_hbm, mask_hbm, length_hbm, emb_hbm, out_ref,
           hidden, gain, target_row, mask, length, emb, X, part, R,
           load_sem, xr, pr, xs, rs, rr):
    width = hidden.shape[1]
    voc = emb.shape[0]
    q, c = lax.axis_index("req"), lax.axis_index("tp")
    x, y, z = q % 2, (q // 2) % 2, q // 4
    half = z // 2
    order = (z, z + 1 - 2 * (z % 2), 2 - half, 3 - 3 * half)

    def device(nz, fa, fb, core):
        fx, fy = fa * (1 - c) + fb * c, fb * (1 - c) + fa * c
        nx, ny = x + fx * (1 - 2 * x), y + fy * (1 - 2 * y)
        return (nz * 4 + ny * 2 + nx, core)

    column = [device(order[i], 0, 0, c) for i in range(4)]
    a_side, b_side, partner = device(z, 1, 0, c), device(z, 0, 1, c), device(z, 0, 0, 1 - c)
    diagonal = device(z, 1, 1, c)
    near = column[1:] + [a_side, b_side, diagonal, partner]

    barrier = pltpu.get_barrier_semaphore()
    loads = [pltpu.make_async_copy(src, dst, load_sem.at[i]) for i, (src, dst) in enumerate(
        ((hidden_hbm, hidden), (gain_hbm, gain), (target_hbm, target_row), (mask_hbm, mask),
         (length_hbm, length), (emb_hbm, emb)))]
    for copy in loads[:3]:
        copy.start()
    for d in near:
        pl.semaphore_signal(barrier, inc=1, device_id=d, device_id_type=MESH)
    for copy in loads[3:]:
        copy.start()
    for copy in loads[:3]:
        copy.wait()
    rows = hidden[...].astype(jnp.float32)
    scale = lax.rsqrt(jnp.mean(rows * rows, axis=1, keepdims=True) + 1e-06)
    own = pl.ds(pl.multiple_of(z * 8 * slots, slots), slots)
    X[own, 0:width] = (rows * scale * gain[...]).astype(jnp.bfloat16)
    tgt = jnp.broadcast_to(target_row[...], (slots, slots))
    eye = lax.broadcasted_iota(jnp.int32, (slots, slots), 0) == lax.broadcasted_iota(
        jnp.int32, (slots, slots), 1)
    tcol = jnp.sum(jnp.where(eye, tgt, 0).astype(jnp.float32), axis=1, keepdims=True)
    high = jnp.floor(tcol * (1.0 / 256.0))
    low = tcol - high * 256.0
    lane = lax.broadcasted_iota(jnp.int32, (slots, 128), 1)
    X[own, width:width + 128] = jnp.where(
        lane == 0, high, jnp.where(lane == 1, low, 0.0)).astype(jnp.bfloat16)
    pl.semaphore_wait(barrier, len(near))

    def block(slot, n=1):
        return X.at[pl.ds(pl.multiple_of(slot * slots, slots), n * slots), :]

    def copy_of(src, dst, recv_sem, dev):
        return pltpu.make_async_remote_copy(
            src_ref=block(src), dst_ref=block(dst), send_sem=xs,
            recv_sem=recv_sem, device_id=dev, device_id_type=MESH)

    def sem_of(b, a, s):
        return xr.at[s * 4 + b * 2 + a]

    def send(b, a, i, way):
        s = order[i]
        to = {"a": (b, 1), "b": (1, a), "d": (1, 1)}.get(way, (b, a))
        dev = {"a": a_side, "b": b_side, "d": diagonal}[way] if way in ("a", "b", "d") else column[way]
        copy_of(J(b, a, 0, s), J(*to, 0, s), sem_of(*to, s), dev).start()

    def to_partner(b, a, i):
        copy_of(J(b, a, 0, order[i]), J(b, a, 1, order[i]), pr.at[i // 2], partner).start()

    def arrived(b, a, i):
        slot = J(b, a, 0, order[i])
        copy_of(slot, slot, sem_of(b, a, order[i]), partner).wait_recv()

    def partner_arrived(g, n):
        pltpu.make_async_remote_copy(
            src_ref=block(0, n), dst_ref=block(0, n), send_sem=xs, recv_sem=pr.at[g],
            device_id=partner, device_id_type=MESH).wait_recv()

    def steps(plan, own_given=False):
        for k, step in enumerate(plan):
            if len(step) == 4:
                send(*step)
                continue
            if not own_given:
                to_partner(0, 0, 0)
                own_given = True
            arrived(*step)
            to_give.append(step)
            if k + 1 < len(plan) and len(plan[k + 1]) == 3:
                flush()
        flush()

    to_give = []

    def flush():
        while to_give:
            to_partner(*to_give.pop(0))

    start = ((q * 2 + c) * voc).astype(jnp.float32)
    pick = lax.broadcasted_iota(jnp.int32, (8, 128), 1)
    pick = jnp.where(pick == 0, 256.0, jnp.where(pick == 1, 1.0, 0.0)).astype(jnp.bfloat16)

    def compute(base, toks, dst):
        rows = pl.ds(pl.multiple_of(base, 128), toks)
        target = lax.dot_general(
            pick, X[rows, width:width + 128], (((1,), (1,)), ((), ())),
            preferred_element_type=jnp.float32)[0:1, :] - start
        raw = lax.dot_general(
            emb[...], X[rows, 0:width], (((1,), (1,)), ((), ())),
            preferred_element_type=jnp.float32)
        soft = jnp.tanh(raw * (1.0 / 30.0))
        expo = jnp.exp2(soft * EXP2)
        ident = lax.broadcasted_iota(jnp.int32, (voc, toks), 0).astype(jnp.float32)
        sums = (jnp.sum(expo, axis=0, keepdims=True),
                30.0 * jnp.sum(expo * soft, axis=0, keepdims=True),
                30.0 * jnp.sum(jnp.where(ident == target, soft, 0.0), axis=0, keepdims=True),
                jnp.zeros((1, toks), jnp.float32))
        for h in range(toks // (8 * slots)):
            for r in range(4):
                part[dst + h, r:r + 1, :] = sums[r][:, h * 8 * slots:(h + 1) * 8 * slots]

    def sent(n):
        pltpu.make_async_remote_copy(
            src_ref=block(0, n), dst_ref=block(0, n), send_sem=xs, recv_sem=rr,
            device_id=partner, device_id_type=MESH).wait_send()

    def give(i):
        for k in range(7, -1, -1):
            if i + k == 0:
                continue
            b, a, area = k // 4, k // 2 % 2, k % 2
            fa, fb = (a, b) if area == 0 else (b, a)
            pltpu.make_async_remote_copy(
                src_ref=part.at[order[i]], dst_ref=R.at[z * 8 + k], send_sem=rs, recv_sem=rr,
                device_id=device(order[i], fa, fb, c if area == 0 else 1 - c),
                device_id_type=MESH).start()

    mid = (z + 1) // 2 % 2

    @pl.when(mid == 0)
    def _():
        steps(END[:SPLIT[0]])

    @pl.when(mid == 1)
    def _():
        steps(MID[:SPLIT[1]])

    loads[5].wait()
    partner_arrived(0, 8)
    compute(half * 16 * slots, 16 * slots, half * 2)
    give(0)
    give(1)

    @pl.when(mid == 0)
    def _():
        steps(END[SPLIT[0]:], True)

    @pl.when(mid == 1)
    def _():
        steps(MID[SPLIT[1]:], True)

    partner_arrived(1, 8)
    compute((1 - half) * 16 * slots, 16 * slots, (1 - half) * 2)
    give(3)
    give(2)

    @pl.when(mid == 0)
    def _():
        sent(SENDS[0])

    @pl.when(mid == 1)
    def _():
        sent(SENDS[1])

    gathered = pltpu.make_async_remote_copy(
        src_ref=R.at[pl.ds(0, 31)], dst_ref=R.at[pl.ds(0, 31)], send_sem=rs, recv_sem=rr,
        device_id=partner, device_id_type=MESH)
    gathered.wait_send()
    gathered.wait_recv()
    R[z * 8] = part[z]
    home = lax.broadcasted_iota(jnp.int32, (4, 8 * slots), 1) // slots
    acc = jnp.zeros((4, 8 * slots), jnp.float32)
    for k in range(8):
        acc = acc + jnp.where(home == k, (R[k] + R[8 + k]) + (R[16 + k] + R[24 + k]), 0.0)
    for shift in (64, 32, 16):
        acc = acc + pltpu.roll(acc, shift, 1)
    total, moment, picked = (acc[i:i + 1, 0:slots] for i in range(3))
    lse = jnp.log(total)
    position = c * slots + lax.broadcasted_iota(jnp.int32, (1, slots), 1)
    for copy in loads[3:5]:
        copy.wait()
    scored = (mask[...] == 1) & (position < length[...])
    out_ref[0:1, :] = jnp.where(scored, picked - lse, 0.0)
    out_ref[1:2, :] = jnp.where(scored, lse - moment / total, 0.0)


def fused(hidden, norm_gain, embedding, target_ids, lengths, response_mask):
    _, slots, width = hidden.shape
    voc = embedding.shape[0]
    anywhere = pl.BlockSpec(memory_space=pl.ANY)
    dma = pltpu.SemaphoreType.DMA
    out = pl.pallas_call(
        functools.partial(kernel, slots),
        out_shape=pltpu.VMEM((2, slots), jnp.float32),
        in_specs=[anywhere] * 6,
        out_specs=pl.BlockSpec(memory_space=pltpu.VMEM),
        scratch_shapes=[
            pltpu.VMEM((slots, width), jnp.bfloat16),
            pltpu.VMEM((1, width), jnp.float32),
            pltpu.VMEM((1, slots), jnp.int32),
            pltpu.VMEM((1, slots), jnp.int32),
            pltpu.VMEM((1, 1), jnp.int32),
            pltpu.VMEM((voc, width), jnp.bfloat16),
            pltpu.VMEM((32 * slots, width + 128), jnp.bfloat16),
            pltpu.VMEM((4, 4, 8 * slots), jnp.float32),
            pltpu.VMEM((32, 4, 8 * slots), jnp.float32),
            dma((6,)), dma((16,)), dma((3,)), dma, dma, dma,
        ],
        compiler_params=pltpu.CompilerParams(collective_id=0, has_side_effects=True),
    )(hidden.reshape(slots, width), norm_gain.reshape(1, width), target_ids, response_mask,
      lengths.reshape(1, 1), embedding)
    return (out[0:1], out[1:2])


def solution(mesh):
    body = fused if dict(mesh.shape) == {"req": 16, "tp": 2} else on_device
    return jax.shard_map(body, mesh=mesh, **SPECS)
```

```python
import functools
import math

import jax
import jax.numpy as jnp
from jax import lax
from jax.experimental import pallas as pl
from jax.experimental.pallas import tpu as pltpu
from jax.sharding import PartitionSpec as P

MESH = pl.DeviceIdType.MESH
SPECS = dict(
    in_specs=(
        P("req", "tp", None),
        P(),
        P(("req", "tp"), None),
        P("req", "tp"),
        P("req"),
        P("req", "tp"),
    ),
    out_specs=(P("req", "tp"), P("req", "tp")),
    check_vma=False,
)


def vocab_sums(states, targets, table, vocab_start):
    raw = lax.dot_general(
        states, table, (((1,), (1,)), ((), ())), preferred_element_type=jnp.float32
    )
    logits = 30.0 * jnp.tanh(raw / 30.0)
    expo = jnp.exp(logits)
    ident = vocab_start + lax.broadcasted_iota(jnp.int32, (1, table.shape[0]), 1)
    hit = jnp.where(ident == targets[:, None], logits, jnp.float32(0.0))
    return (jnp.sum(expo, axis=1), jnp.sum(expo * logits, axis=1), jnp.sum(hit, axis=1))


def on_device(hidden, norm_gain, embedding, target_ids, lengths, response_mask):
    seq_here, slots, width = hidden.shape
    rows = hidden.reshape(seq_here * slots, width).astype(jnp.float32)
    scale = lax.rsqrt(jnp.mean(rows * rows, axis=1, keepdims=True) + 1e-06)
    normed = (rows * scale * norm_gain[None, :]).astype(jnp.bfloat16)
    targets = target_ids.reshape(seq_here * slots)
    vocab_start = lax.axis_index(("req", "tp")) * embedding.shape[0]
    sums = vocab_sums(
        lax.all_gather(normed, ("req", "tp"), axis=0, tiled=True),
        lax.all_gather(targets, ("req", "tp"), axis=0, tiled=True),
        embedding,
        vocab_start,
    )
    total, moment, picked = (
        lax.psum_scatter(s, ("req", "tp"), scatter_dimension=0, tiled=True) for s in sums
    )
    lse = jnp.log(total)
    position = lax.axis_index("tp") * slots + lax.broadcasted_iota(jnp.int32, (seq_here, slots), 1)
    scored = (response_mask == 1) & (position < lengths[:, None])
    logprob = jnp.where(scored, (picked - lse).reshape(seq_here, slots), jnp.float32(0.0))
    entropy = jnp.where(scored, (lse - moment / total).reshape(seq_here, slots), jnp.float32(0.0))
    return (logprob, entropy)


EXP2 = 30.0 / math.log(2.0)

END = (
    (0, 0, 0, "a"), (0, 0, 0, "b"), (0, 0, 0, 2), (0, 0, 0, "d"), (0, 0, 0, 1), (0, 1, 0),
    (0, 0, 1), (0, 0, 1, "d"), (1, 0, 0), (1, 0, 0, 1), (0, 0, 1, "b"), (0, 0, 2),
    (0, 0, 2, "a"), (0, 0, 2, "b"), (0, 0, 2, 1), (1, 1, 0), (1, 1, 1), (1, 1, 1, 2), (0, 0, 3),
    (0, 0, 3, "d"), (1, 0, 1), (0, 1, 2), (0, 1, 2, "b"), (1, 0, 2), (0, 1, 1), (1, 0, 3),
    (1, 1, 3), (1, 1, 2), (0, 1, 3),
)
MID = (
    (0, 0, 0, 1), (0, 0, 0, "b"), (0, 0, 0, "a"), (0, 0, 0, 3), (1, 0, 0), (1, 0, 0, "a"),
    (0, 1, 0), (0, 1, 0, 2), (0, 0, 3), (0, 0, 3, 1), (0, 0, 3, "b"), (0, 1, 0, 1),
    (1, 0, 0, 2), (0, 0, 1), (0, 0, 1, "a"), (1, 1, 0), (0, 0, 3, "a"), (1, 0, 3), (1, 0, 3, 1),
    (0, 1, 2), (1, 0, 1), (1, 0, 1, "a"), (0, 1, 1), (1, 0, 2), (0, 1, 3), (0, 1, 3, 1),
    (1, 0, 3, "a"), (0, 0, 2), (1, 1, 1), (1, 1, 2), (1, 1, 3),
)
SPLIT = (25, 29)
SENDS = (30, 32)


def J(b, a, area, s):
    return s * 8 + b * 4 + a * 2 + area


def kernel(slots, hidden_hbm, gain_hbm, target_hbm, mask_hbm, length_hbm, emb_hbm, out_ref,
           hidden, gain, target_row, mask, length, emb, X, part, R,
           load_sem, xr, pr, xs, rs, rr):
    width = hidden.shape[1]
    voc = emb.shape[0]
    q, c = lax.axis_index("req"), lax.axis_index("tp")
    x, y, z = q % 2, (q // 2) % 2, q // 4
    half = z // 2
    order = (z, z + 1 - 2 * (z % 2), 2 - half, 3 - 3 * half)

    def device(nz, fa, fb, core):
        fx, fy = fa * (1 - c) + fb * c, fb * (1 - c) + fa * c
        nx, ny = x + fx * (1 - 2 * x), y + fy * (1 - 2 * y)
        return (nz * 4 + ny * 2 + nx, core)

    column = [device(order[i], 0, 0, c) for i in range(4)]
    a_side, b_side, partner = device(z, 1, 0, c), device(z, 0, 1, c), device(z, 0, 0, 1 - c)
    diagonal = device(z, 1, 1, c)
    near = column[1:] + [a_side, b_side, diagonal, partner]

    barrier = pltpu.get_barrier_semaphore()
    loads = [pltpu.make_async_copy(src, dst, load_sem.at[i]) for i, (src, dst) in enumerate(
        ((hidden_hbm, hidden), (gain_hbm, gain), (target_hbm, target_row), (mask_hbm, mask),
         (length_hbm, length), (emb_hbm, emb)))]
    for copy in loads[:3]:
        copy.start()
    for d in near:
        pl.semaphore_signal(barrier, inc=1, device_id=d, device_id_type=MESH)
    for copy in loads[3:]:
        copy.start()
    for copy in loads[:3]:
        copy.wait()
    rows = hidden[...].astype(jnp.float32)
    scale = lax.rsqrt(jnp.mean(rows * rows, axis=1, keepdims=True) + 1e-06)
    own = pl.ds(pl.multiple_of(z * 8 * slots, slots), slots)
    X[own, 0:width] = (rows * scale * gain[...]).astype(jnp.bfloat16)
    tgt = jnp.broadcast_to(target_row[...], (slots, slots))
    eye = lax.broadcasted_iota(jnp.int32, (slots, slots), 0) == lax.broadcasted_iota(
        jnp.int32, (slots, slots), 1)
    tcol = jnp.sum(jnp.where(eye, tgt, 0).astype(jnp.float32), axis=1, keepdims=True)
    high = jnp.floor(tcol * (1.0 / 256.0))
    low = tcol - high * 256.0
    lane = lax.broadcasted_iota(jnp.int32, (slots, 128), 1)
    X[own, width:width + 128] = jnp.where(
        lane == 0, high, jnp.where(lane == 1, low, 0.0)).astype(jnp.bfloat16)
    pl.semaphore_wait(barrier, len(near))

    def block(slot, n=1):
        return X.at[pl.ds(pl.multiple_of(slot * slots, slots), n * slots), :]

    def copy_of(src, dst, recv_sem, dev):
        return pltpu.make_async_remote_copy(
            src_ref=block(src), dst_ref=block(dst), send_sem=xs,
            recv_sem=recv_sem, device_id=dev, device_id_type=MESH)

    def sem_of(b, a, s):
        return xr.at[s * 4 + b * 2 + a]

    def send(b, a, i, way):
        s = order[i]
        to = {"a": (b, 1), "b": (1, a), "d": (1, 1)}.get(way, (b, a))
        dev = {"a": a_side, "b": b_side, "d": diagonal}[way] if way in ("a", "b", "d") else column[way]
        copy_of(J(b, a, 0, s), J(*to, 0, s), sem_of(*to, s), dev).start()

    def to_partner(b, a, i):
        copy_of(J(b, a, 0, order[i]), J(b, a, 1, order[i]), pr.at[i // 2], partner).start()

    def arrived(b, a, i):
        slot = J(b, a, 0, order[i])
        copy_of(slot, slot, sem_of(b, a, order[i]), partner).wait_recv()

    def partner_arrived(g, n):
        pltpu.make_async_remote_copy(
            src_ref=block(0, n), dst_ref=block(0, n), send_sem=xs, recv_sem=pr.at[g],
            device_id=partner, device_id_type=MESH).wait_recv()

    def steps(plan, own_given=False):
        for k, step in enumerate(plan):
            if len(step) == 4:
                send(*step)
                continue
            if not own_given:
                to_partner(0, 0, 0)
                own_given = True
            arrived(*step)
            to_give.append(step)
            if k + 1 < len(plan) and len(plan[k + 1]) == 3:
                flush()
        flush()

    to_give = []

    def flush():
        while to_give:
            to_partner(*to_give.pop(0))

    start = ((q * 2 + c) * voc).astype(jnp.float32)
    pick = lax.broadcasted_iota(jnp.int32, (8, 128), 1)
    pick = jnp.where(pick == 0, 256.0, jnp.where(pick == 1, 1.0, 0.0)).astype(jnp.bfloat16)

    def compute(base, toks, dst):
        rows = pl.ds(pl.multiple_of(base, 128), toks)
        target = lax.dot_general(
            pick, X[rows, width:width + 128], (((1,), (1,)), ((), ())),
            preferred_element_type=jnp.float32)[0:1, :] - start
        def table_rows(v, sums):
            first = pl.multiple_of(v * 256, 256)
            raw = lax.dot_general(
                emb[pl.ds(first, 256), :], X[rows, 0:width], (((1,), (1,)), ((), ())),
                preferred_element_type=jnp.float32)
            soft = jnp.tanh(raw * (1.0 / 30.0))
            expo = jnp.exp2(soft * EXP2)
            ident = lax.broadcasted_iota(jnp.int32, (256, toks), 0) + first
            hit = ident.astype(jnp.float32) == target
            return tuple(old + jnp.sum(new, axis=0, keepdims=True) for old, new in zip(
                sums, (expo, expo * soft, jnp.where(hit, soft, 0.0))))

        zero = jnp.zeros((1, toks), jnp.float32)
        total, moment, picked = lax.fori_loop(0, voc // 256, table_rows, (zero,) * 3)
        sums = (total, 30.0 * moment, 30.0 * picked, zero)
        for h in range(toks // (8 * slots)):
            for r in range(4):
                part[dst + h, r:r + 1, :] = sums[r][:, h * 8 * slots:(h + 1) * 8 * slots]

    def sent(n):
        pltpu.make_async_remote_copy(
            src_ref=block(0, n), dst_ref=block(0, n), send_sem=xs, recv_sem=rr,
            device_id=partner, device_id_type=MESH).wait_send()

    def give(i):
        for k in range(7, -1, -1):
            if i + k == 0:
                continue
            b, a, area = k // 4, k // 2 % 2, k % 2
            fa, fb = (a, b) if area == 0 else (b, a)
            pltpu.make_async_remote_copy(
                src_ref=part.at[order[i]], dst_ref=R.at[z * 8 + k], send_sem=rs, recv_sem=rr,
                device_id=device(order[i], fa, fb, c if area == 0 else 1 - c),
                device_id_type=MESH).start()

    mid = (z + 1) // 2 % 2

    @pl.when(mid == 0)
    def _():
        steps(END[:SPLIT[0]])

    @pl.when(mid == 1)
    def _():
        steps(MID[:SPLIT[1]])

    loads[5].wait()
    partner_arrived(0, 8)
    compute(half * 16 * slots, 16 * slots, half * 2)

    @pl.when(mid == 0)
    def _():
        steps(END[SPLIT[0]:], True)

    @pl.when(mid == 1)
    def _():
        steps(MID[SPLIT[1]:], True)

    give(0)
    give(1)
    partner_arrived(1, 8)
    compute((1 - half) * 16 * slots, 16 * slots, (1 - half) * 2)
    give(3)
    give(2)

    @pl.when(mid == 0)
    def _():
        sent(SENDS[0])

    @pl.when(mid == 1)
    def _():
        sent(SENDS[1])

    gathered = pltpu.make_async_remote_copy(
        src_ref=R.at[pl.ds(0, 31)], dst_ref=R.at[pl.ds(0, 31)], send_sem=rs, recv_sem=rr,
        device_id=partner, device_id_type=MESH)
    gathered.wait_send()
    gathered.wait_recv()
    R[z * 8] = part[z]
    home = lax.broadcasted_iota(jnp.int32, (4, 8 * slots), 1) // slots
    acc = jnp.zeros((4, 8 * slots), jnp.float32)
    for k in range(8):
        acc = acc + jnp.where(home == k, (R[k] + R[8 + k]) + (R[16 + k] + R[24 + k]), 0.0)
    for shift in (64, 32, 16):
        acc = acc + pltpu.roll(acc, shift, 1)
    total, moment, picked = (acc[i:i + 1, 0:slots] for i in range(3))
    lse = jnp.log(total)
    position = c * slots + lax.broadcasted_iota(jnp.int32, (1, slots), 1)
    for copy in loads[3:5]:
        copy.wait()
    scored = (mask[...] == 1) & (position < length[...])
    out_ref[0:1, :] = jnp.where(scored, picked - lse, 0.0)
    out_ref[1:2, :] = jnp.where(scored, lse - moment / total, 0.0)


def fused(hidden, norm_gain, embedding, target_ids, lengths, response_mask):
    _, slots, width = hidden.shape
    voc = embedding.shape[0]
    anywhere = pl.BlockSpec(memory_space=pl.ANY)
    dma = pltpu.SemaphoreType.DMA
    out = pl.pallas_call(
        functools.partial(kernel, slots),
        out_shape=pltpu.VMEM((2, slots), jnp.float32),
        in_specs=[anywhere] * 6,
        out_specs=pl.BlockSpec(memory_space=pltpu.VMEM),
        scratch_shapes=[
            pltpu.VMEM((slots, width), jnp.bfloat16),
            pltpu.VMEM((1, width), jnp.float32),
            pltpu.VMEM((1, slots), jnp.int32),
            pltpu.VMEM((1, slots), jnp.int32),
            pltpu.VMEM((1, 1), jnp.int32),
            pltpu.VMEM((voc, width), jnp.bfloat16),
            pltpu.VMEM((32 * slots, width + 128), jnp.bfloat16),
            pltpu.VMEM((4, 4, 8 * slots), jnp.float32),
            pltpu.VMEM((32, 4, 8 * slots), jnp.float32),
            dma((6,)), dma((16,)), dma((3,)), dma, dma, dma,
        ],
        compiler_params=pltpu.CompilerParams(collective_id=0, has_side_effects=True),
    )(hidden.reshape(slots, width), norm_gain.reshape(1, width), target_ids, response_mask,
      lengths.reshape(1, 1), embedding)
    return (out[0:1], out[1:2])


def solution(mesh):
    body = fused if dict(mesh.shape) == {"req": 16, "tp": 2} else on_device
    return jax.shard_map(body, mesh=mesh, **SPECS)
```

```python
import functools
import math

import jax
import jax.numpy as jnp
from jax import lax
from jax.experimental import pallas as pl
from jax.experimental.pallas import tpu as pltpu
from jax.sharding import PartitionSpec as P

MESH = pl.DeviceIdType.MESH
SPECS = dict(
    in_specs=(
        P("req", "tp", None),
        P(),
        P(("req", "tp"), None),
        P("req", "tp"),
        P("req"),
        P("req", "tp"),
    ),
    out_specs=(P("req", "tp"), P("req", "tp")),
    check_vma=False,
)


def vocab_sums(states, targets, table, vocab_start):
    raw = lax.dot_general(
        states, table, (((1,), (1,)), ((), ())), preferred_element_type=jnp.float32
    )
    logits = 30.0 * jnp.tanh(raw / 30.0)
    expo = jnp.exp(logits)
    ident = vocab_start + lax.broadcasted_iota(jnp.int32, (1, table.shape[0]), 1)
    hit = jnp.where(ident == targets[:, None], logits, jnp.float32(0.0))
    return (jnp.sum(expo, axis=1), jnp.sum(expo * logits, axis=1), jnp.sum(hit, axis=1))


def on_device(hidden, norm_gain, embedding, target_ids, lengths, response_mask):
    seq_here, slots, width = hidden.shape
    rows = hidden.reshape(seq_here * slots, width).astype(jnp.float32)
    scale = lax.rsqrt(jnp.mean(rows * rows, axis=1, keepdims=True) + 1e-06)
    normed = (rows * scale * norm_gain[None, :]).astype(jnp.bfloat16)
    targets = target_ids.reshape(seq_here * slots)
    vocab_start = lax.axis_index(("req", "tp")) * embedding.shape[0]
    sums = vocab_sums(
        lax.all_gather(normed, ("req", "tp"), axis=0, tiled=True),
        lax.all_gather(targets, ("req", "tp"), axis=0, tiled=True),
        embedding,
        vocab_start,
    )
    total, moment, picked = (
        lax.psum_scatter(s, ("req", "tp"), scatter_dimension=0, tiled=True) for s in sums
    )
    lse = jnp.log(total)
    position = lax.axis_index("tp") * slots + lax.broadcasted_iota(jnp.int32, (seq_here, slots), 1)
    scored = (response_mask == 1) & (position < lengths[:, None])
    logprob = jnp.where(scored, (picked - lse).reshape(seq_here, slots), jnp.float32(0.0))
    entropy = jnp.where(scored, (lse - moment / total).reshape(seq_here, slots), jnp.float32(0.0))
    return (logprob, entropy)


EXP2 = 30.0 / math.log(2.0)

END = (
    (0, 0, 0, "a"), (0, 0, 0, "b"), (0, 0, 0, 2), (0, 0, 0, "d"), (0, 0, 0, 1), (0, 1, 0),
    (0, 0, 1), (0, 0, 1, "d"), (1, 0, 0), (1, 0, 0, 1), (0, 0, 1, "b"), (0, 0, 2),
    (0, 0, 2, "a"), (0, 0, 2, "b"), (0, 0, 2, 1), (1, 1, 0), (1, 1, 1), (1, 1, 1, 2), (0, 0, 3),
    (0, 0, 3, "d"), (1, 0, 1), (0, 1, 2), (0, 1, 2, "b"), (1, 0, 2), (0, 1, 1), (1, 0, 3),
    (1, 1, 3), (1, 1, 2), (0, 1, 3),
)
MID = (
    (0, 0, 0, 1), (0, 0, 0, "b"), (0, 0, 0, "a"), (0, 0, 0, 3), (1, 0, 0), (1, 0, 0, "a"),
    (0, 1, 0), (0, 1, 0, 2), (0, 0, 3), (0, 0, 3, 1), (0, 0, 3, "b"), (0, 1, 0, 1),
    (1, 0, 0, 2), (0, 0, 1), (0, 0, 1, "a"), (1, 1, 0), (0, 0, 3, "a"), (1, 0, 3), (1, 0, 3, 1),
    (0, 1, 2), (1, 0, 1), (1, 0, 1, "a"), (0, 1, 1), (1, 0, 2), (0, 1, 3), (0, 1, 3, 1),
    (1, 0, 3, "a"), (0, 0, 2), (1, 1, 1), (1, 1, 2), (1, 1, 3),
)
SPLIT = (25, 29)
SENDS = (30, 32)


def J(b, a, area, s):
    return s * 8 + b * 4 + a * 2 + area


def kernel(slots, hidden_hbm, gain_hbm, target_hbm, mask_hbm, length_hbm, emb_hbm, out_ref,
           hidden, gain, target_row, mask, length, emb, X, part, R,
           load_sem, xr, pr, xs, rs, rr):
    width = hidden.shape[1]
    voc = emb.shape[0]
    q, c = lax.axis_index("req"), lax.axis_index("tp")
    x, y, z = q % 2, (q // 2) % 2, q // 4
    half = z // 2
    order = (z, z + 1 - 2 * (z % 2), 2 - half, 3 - 3 * half)

    def device(nz, fa, fb, core):
        fx, fy = fa * (1 - c) + fb * c, fb * (1 - c) + fa * c
        nx, ny = x + fx * (1 - 2 * x), y + fy * (1 - 2 * y)
        return (nz * 4 + ny * 2 + nx, core)

    column = [device(order[i], 0, 0, c) for i in range(4)]
    a_side, b_side, partner = device(z, 1, 0, c), device(z, 0, 1, c), device(z, 0, 0, 1 - c)
    diagonal = device(z, 1, 1, c)
    near = column[1:] + [a_side, b_side, diagonal, partner]

    barrier = pltpu.get_barrier_semaphore()
    loads = [pltpu.make_async_copy(src, dst, load_sem.at[i]) for i, (src, dst) in enumerate(
        ((hidden_hbm, hidden), (gain_hbm, gain), (target_hbm, target_row), (mask_hbm, mask),
         (length_hbm, length), (emb_hbm, emb)))]
    for copy in loads[:3]:
        copy.start()
    for d in near:
        pl.semaphore_signal(barrier, inc=1, device_id=d, device_id_type=MESH)
    for copy in loads[3:]:
        copy.start()
    for copy in loads[:3]:
        copy.wait()
    rows = hidden[...].astype(jnp.float32)
    scale = lax.rsqrt(jnp.mean(rows * rows, axis=1, keepdims=True) + 1e-06)
    own = pl.ds(pl.multiple_of(z * 8 * slots, slots), slots)
    X[own, 0:width] = (rows * scale * gain[...]).astype(jnp.bfloat16)
    tgt = jnp.broadcast_to(target_row[...], (slots, slots))
    eye = lax.broadcasted_iota(jnp.int32, (slots, slots), 0) == lax.broadcasted_iota(
        jnp.int32, (slots, slots), 1)
    tcol = jnp.sum(jnp.where(eye, tgt, 0).astype(jnp.float32), axis=1, keepdims=True)
    high = jnp.floor(tcol * (1.0 / 256.0))
    low = tcol - high * 256.0
    lane = lax.broadcasted_iota(jnp.int32, (slots, 128), 1)
    X[own, width:width + 128] = jnp.where(
        lane == 0, high, jnp.where(lane == 1, low, 0.0)).astype(jnp.bfloat16)
    pl.semaphore_wait(barrier, len(near))

    def block(slot, n=1):
        return X.at[pl.ds(pl.multiple_of(slot * slots, slots), n * slots), :]

    def copy_of(src, dst, recv_sem, dev):
        return pltpu.make_async_remote_copy(
            src_ref=block(src), dst_ref=block(dst), send_sem=xs,
            recv_sem=recv_sem, device_id=dev, device_id_type=MESH)

    def sem_of(b, a, s):
        return xr.at[s * 4 + b * 2 + a]

    def send(b, a, i, way):
        s = order[i]
        to = {"a": (b, 1), "b": (1, a), "d": (1, 1)}.get(way, (b, a))
        dev = {"a": a_side, "b": b_side, "d": diagonal}[way] if way in ("a", "b", "d") else column[way]
        copy_of(J(b, a, 0, s), J(*to, 0, s), sem_of(*to, s), dev).start()

    def to_partner(b, a, i):
        copy_of(J(b, a, 0, order[i]), J(b, a, 1, order[i]), pr.at[i // 2], partner).start()

    def arrived(b, a, i):
        slot = J(b, a, 0, order[i])
        copy_of(slot, slot, sem_of(b, a, order[i]), partner).wait_recv()

    def partner_arrived(g, n):
        pltpu.make_async_remote_copy(
            src_ref=block(0, n), dst_ref=block(0, n), send_sem=xs, recv_sem=pr.at[g],
            device_id=partner, device_id_type=MESH).wait_recv()

    def steps(plan, own_given=False):
        for k, step in enumerate(plan):
            if len(step) == 4:
                send(*step)
                continue
            if not own_given:
                to_partner(0, 0, 0)
                own_given = True
            arrived(*step)
            to_give.append(step)
            if k + 1 < len(plan) and len(plan[k + 1]) == 3:
                flush()
        flush()

    to_give = []

    def flush():
        while to_give:
            to_partner(*to_give.pop(0))

    start = ((q * 2 + c) * voc).astype(jnp.float32)
    pick = lax.broadcasted_iota(jnp.int32, (8, 128), 1)
    pick = jnp.where(pick == 0, 256.0, jnp.where(pick == 1, 1.0, 0.0)).astype(jnp.bfloat16)

    def compute(base, toks, dst):
        rows = pl.ds(pl.multiple_of(base, 128), toks)
        target = lax.dot_general(
            pick, X[rows, width:width + 128], (((1,), (1,)), ((), ())),
            preferred_element_type=jnp.float32)[0:1, :] - start
        def table_rows(v, sums):
            first = pl.multiple_of(v * 256, 256)
            raw = lax.dot_general(
                emb[pl.ds(first, 256), :], X[rows, 0:width], (((1,), (1,)), ((), ())),
                preferred_element_type=jnp.float32)
            soft = jnp.tanh(raw * (1.0 / 30.0))
            expo = jnp.exp2(soft * EXP2)
            ident = lax.broadcasted_iota(jnp.int32, (256, toks), 0) + first
            hit = ident.astype(jnp.float32) == target
            return tuple(old + jnp.sum(new, axis=0, keepdims=True) for old, new in zip(
                sums, (expo, expo * soft, jnp.where(hit, soft, 0.0))))

        zero = jnp.zeros((1, toks), jnp.float32)
        total, moment, picked = lax.fori_loop(0, voc // 256, table_rows, (zero,) * 3)
        sums = (total, 30.0 * moment, 30.0 * picked, zero)
        for h in range(toks // (8 * slots)):
            for r in range(4):
                part[dst + h, r:r + 1, :] = sums[r][:, h * 8 * slots:(h + 1) * 8 * slots]

    def sent(n):
        pltpu.make_async_remote_copy(
            src_ref=block(0, n), dst_ref=block(0, n), send_sem=xs, recv_sem=rr,
            device_id=partner, device_id_type=MESH).wait_send()

    def give(i):
        for k in range(7, -1, -1):
            if i + k == 0:
                continue
            b, a, area = k // 4, k // 2 % 2, k % 2
            fa, fb = (a, b) if area == 0 else (b, a)
            pltpu.make_async_remote_copy(
                src_ref=part.at[order[i]], dst_ref=R.at[z * 8 + k], send_sem=rs, recv_sem=rr,
                device_id=device(order[i], fa, fb, c if area == 0 else 1 - c),
                device_id_type=MESH).start()

    mid = (z + 1) // 2 % 2

    @pl.when(mid == 0)
    def _():
        steps(END[:SPLIT[0]])

    @pl.when(mid == 1)
    def _():
        steps(MID[:SPLIT[1]])

    for copy in loads[3:]:
        copy.wait()
    partner_arrived(0, 8)
    compute(half * 16 * slots, 16 * slots, half * 2)

    @pl.when(mid == 0)
    def _():
        steps(END[SPLIT[0]:], True)

    @pl.when(mid == 1)
    def _():
        steps(MID[SPLIT[1]:], True)

    give(0)
    give(1)
    partner_arrived(1, 8)
    compute((1 - half) * 16 * slots, 16 * slots, (1 - half) * 2)
    give(3)
    give(2)

    @pl.when(mid == 0)
    def _():
        sent(SENDS[0])

    @pl.when(mid == 1)
    def _():
        sent(SENDS[1])

    gathered = pltpu.make_async_remote_copy(
        src_ref=R.at[pl.ds(0, 31)], dst_ref=R.at[pl.ds(0, 31)], send_sem=rs, recv_sem=rr,
        device_id=partner, device_id_type=MESH)
    R[z * 8] = part[z]
    gathered.wait_send()
    gathered.wait_recv()
    home = lax.broadcasted_iota(jnp.int32, (4, 8 * slots), 1) // slots
    acc = jnp.zeros((4, 8 * slots), jnp.float32)
    for k in range(8):
        acc = acc + jnp.where(home == k, (R[k] + R[8 + k]) + (R[16 + k] + R[24 + k]), 0.0)
    for shift in (64, 32, 16):
        acc = acc + pltpu.roll(acc, shift, 1)
    total, moment, picked = (acc[i:i + 1, 0:slots] for i in range(3))
    lse = jnp.log(total)
    position = c * slots + lax.broadcasted_iota(jnp.int32, (1, slots), 1)
    scored = (mask[...] == 1) & (position < length[...])
    out_ref[0:1, :] = jnp.where(scored, picked - lse, 0.0)
    out_ref[1:2, :] = jnp.where(scored, lse - moment / total, 0.0)


def fused(hidden, norm_gain, embedding, target_ids, lengths, response_mask):
    _, slots, width = hidden.shape
    voc = embedding.shape[0]
    anywhere = pl.BlockSpec(memory_space=pl.ANY)
    dma = pltpu.SemaphoreType.DMA
    out = pl.pallas_call(
        functools.partial(kernel, slots),
        out_shape=pltpu.VMEM((2, slots), jnp.float32),
        in_specs=[anywhere] * 6,
        out_specs=pl.BlockSpec(memory_space=pltpu.VMEM),
        scratch_shapes=[
            pltpu.VMEM((slots, width), jnp.bfloat16),
            pltpu.VMEM((1, width), jnp.float32),
            pltpu.VMEM((1, slots), jnp.int32),
            pltpu.VMEM((1, slots), jnp.int32),
            pltpu.VMEM((1, 1), jnp.int32),
            pltpu.VMEM((voc, width), jnp.bfloat16),
            pltpu.VMEM((32 * slots, width + 128), jnp.bfloat16),
            pltpu.VMEM((4, 4, 8 * slots), jnp.float32),
            pltpu.VMEM((32, 4, 8 * slots), jnp.float32),
            dma((6,)), dma((16,)), dma((3,)), dma, dma, dma,
        ],
        compiler_params=pltpu.CompilerParams(collective_id=0, has_side_effects=True),
    )(hidden.reshape(slots, width), norm_gain.reshape(1, width), target_ids, response_mask,
      lengths.reshape(1, 1), embedding)
    return (out[0:1], out[1:2])


def solution(mesh):
    body = fused if dict(mesh.shape) == {"req": 16, "tp": 2} else on_device
    return jax.shard_map(body, mesh=mesh, **SPECS)
```
